32 devices in a mesh: fsdp: 8 (over z, core), rep: 4 (over y, x).
Axes of the slice: x: 2, y: 2, z: 4, core: 2. Of those that a mesh axis runs over, the one named last changes fastest.
Arguments:
- tokens: bfloat16 [4, 2048, 4096], P('rep', 'fsdp'), may hold values from -6 to 6
- cotangent: bfloat16 [4, 2048, 4096], P('rep', 'fsdp'), may hold values from -1.1953125 to 1.1953125
- block_map: int32 [8, 2], replicated, may hold values from 0 to 31
- matching: int32 [4], replicated, may hold values from 0 to 3, as said below
- tiles: bfloat16 [4, 8, 3, 128, 128], P('rep', 'fsdp'), may hold values from -4 to 4
- first_moment: float32 [4, 8, 3, 128, 128], P('rep', 'fsdp'), may hold values from -3 to 3
- second_moment: float32 [4, 8, 3, 128, 128], P('rep', 'fsdp'), may hold values from 0.3 to 3
Outputs:
- new_tiles: bfloat16 [4, 8, 3, 128, 128], P('rep', 'fsdp')
- new_first: float32 [4, 8, 3, 128, 128], P('rep', 'fsdp')
- new_second: float32 [4, 8, 3, 128, 128], P('rep', 'fsdp')
The draws below stay inside these ranges and needn't reach their ends.
Inputs may be any that keep to these rules, and one draw needn't show every extreme that they name: `matching`: replica r is paired with replica r XOR k, for one k of 1 to 3 drawn for the step.
All inputs are finite; a program needn't handle non-finite values.
Results may differ from the reference program's by a relative error of at most 0.0055.
Values may be sent and summed in bfloat16 or wider, within the bound.
No kernel may reach another device: no remote copies, remote signals or barrier semaphores. Data moves between devices by JAX's collectives and lax.ppermute only.
A program may use at most 64 MiB of HBM per device.

```python
import math
import jax
import jax.numpy as jnp
from jax import lax

BLOCK = 128
D = 4096
TOK_DEV = 256
TOKENS = 2048
UNITS = 8
REPS = 4
N_FSDP = 8


def draw_matching(key, part):
    offset = jax.random.randint(key, (), 1, REPS, dtype=jnp.int32)
    return jnp.bitwise_xor(jnp.arange(REPS, dtype=jnp.int32), offset)


def plant(drawn, stream_key, smallest, largest):
    shape = drawn.shape
    spot = [jax.random.randint(jax.random.fold_in(stream_key, axis), (), 0, shape[axis]) for axis in range(len(shape))]
    drawn = drawn.at[tuple(spot)].set(smallest)
    longest = shape.index(max(shape))
    spot[longest] = (spot[longest] + 1) % shape[longest]
    return drawn.at[tuple(spot)].set(largest)


def shard_levels(stream_key, dims, shards, least, largest):
    loudness, own = 1.0, jax.random.fold_in(stream_key, 6)
    for position, shards_of in shards:
        steps = jnp.exp(jax.random.uniform(jax.random.fold_in(own, position), (shards_of,), jnp.float32, least / len(shards), largest / len(shards)))
        loudness = loudness * jnp.repeat(steps, dims[position] // shards_of).reshape([-1 if axis == position else 1 for axis in range(len(dims))])
    return loudness


def normal_values(own_key, shape, scale, reach, cuts=(), held_as=jnp.bfloat16):
    loudness = shard_levels(own_key, shape, cuts, -0.22, 0.18) if cuts else 1.0
    entries = jax.random.normal(own_key, shape, jnp.float32) * scale * loudness
    return jnp.minimum(jnp.maximum(entries, -reach), reach).astype(held_as)


def setup_inputs(seed: int = 0) -> dict:
    seeds = jax.random.split(jax.random.key(seed), 8)
    tokens = normal_values(seeds[0], (REPS, TOKENS, D), 1.0, 6.0, ((0, 4), (1, 8)))
    cotangent = normal_values(seeds[1], (REPS, TOKENS, D), 0.2, 1.1953125, ((0, 4), (1, 8)))
    block_map = plant(jax.random.randint(seeds[2], (UNITS, 2), 0, D // BLOCK), jax.random.fold_in(seeds[2], 1), 0, (D // BLOCK) - 1).astype(jnp.int32)
    matching = draw_matching(jax.random.fold_in(seeds[7], 71), 0)
    tiles = normal_values(seeds[4], (REPS, UNITS, 3, BLOCK, BLOCK), 1.0, 4.0, ((0, 4), (1, 8)))
    first_moment = normal_values(seeds[5], (REPS, UNITS, 3, BLOCK, BLOCK), 0.5, 3.0, ((0, 4), (1, 8)), jnp.float32)
    second_moment = jnp.clip(jnp.exp(math.log(3.0) - 2.3025851 * jax.random.uniform(seeds[6], (REPS, UNITS, 3, BLOCK, BLOCK), jnp.float32) ** shard_levels(seeds[6], (REPS, UNITS, 3, BLOCK, BLOCK), ((0, 4), (1, 8)), -0.2, 0.2)), 0.3, 3.0)
    return {"tokens": tokens, "cotangent": cotangent, "block_map": block_map, "matching": matching, "tiles": tiles, "first_moment": first_moment, "second_moment": second_moment}


def unit_terms(inputs_a, cots_b, weights):
    factor = BLOCK ** (-0.5)
    inputs32 = inputs_a.astype(jnp.float32)
    cots32 = cots_b.astype(jnp.float32)
    weights32 = weights.astype(jnp.float32)
    gate_pre = factor * jnp.einsum('tui,uih->tuh', inputs32, weights32[:, 0])
    up_pre = factor * jnp.einsum('tui,uih->tuh', inputs32, weights32[:, 1])
    sigmoid = jax.nn.sigmoid(gate_pre)
    activated = gate_pre * sigmoid
    hidden = (activated * up_pre).astype(jnp.bfloat16)
    hidden_grad = factor * jnp.einsum('tuo,uho->tuh', cots32, weights32[:, 2])
    gate_grad = (hidden_grad * up_pre * sigmoid * (1.0 + gate_pre * (1.0 - sigmoid))).astype(jnp.bfloat16)
    up_grad = (hidden_grad * activated).astype(jnp.bfloat16)
    gate_term = factor * jnp.einsum('tui,tuh->uih', inputs32, gate_grad.astype(jnp.float32))
    up_term = factor * jnp.einsum('tui,tuh->uih', inputs32, up_grad.astype(jnp.float32))
    down_term = factor * jnp.einsum('tuh,tuo->uho', hidden.astype(jnp.float32), cots32)
    return jnp.stack([gate_term, up_term, down_term], axis=1)

def replica_grads(own_tokens, own_cots, weights, block_map):
    shards_in = own_tokens.reshape(N_FSDP, TOK_DEV, D // BLOCK, BLOCK)
    shards_cot = own_cots.reshape(N_FSDP, TOK_DEV, D // BLOCK, BLOCK)
    first_ids = block_map[:, 0].astype(jnp.int32)
    second_ids = block_map[:, 1].astype(jnp.int32)

    def shard_term(pair):
        inputs_a = jnp.take(pair[0], first_ids, axis=1)
        cots_b = jnp.take(pair[1], second_ids, axis=1)
        return unit_terms(inputs_a, cots_b, weights).astype(jnp.bfloat16)
    terms = lax.map(shard_term, (shards_in, shards_cot))
    return lax.optimization_barrier(jnp.sum(terms.astype(jnp.float32), axis=0))

def reference(tokens, cotangent, block_map, matching, tiles, first_moment, second_moment):
    grads = lax.map(lambda item: replica_grads(item[0], item[1], item[2], block_map), (tokens, cotangent, tiles))
    weights32 = tiles.astype(jnp.float32)
    partner = jnp.take(weights32, matching.astype(jnp.int32), axis=0)
    new_first = 0.9 * first_moment + 0.1 * grads
    new_second = 0.95 * second_moment + 0.05 * grads * grads
    mixed = 0.5 * (weights32 + partner) - 0.02 * (new_first / (jnp.sqrt(new_second) + 1e-08) + 0.1 * weights32)
    return (mixed.astype(jnp.bfloat16), new_first, new_second)
```

```python
import functools

import jax
import jax.numpy as jnp
from jax import lax
from jax.experimental import pallas as pl
from jax.experimental.pallas import tpu as pltpu
from jax.sharding import PartitionSpec as P


BETA_ONE = 0.9
BETA_TWO = 0.95
STEP_RATE = 0.02
WEIGHT_DECAY = 0.1
EPSILON = 1e-08


def exchanged(value, axis, mask):
    pairs = [(source, source ^ mask) for source in range(lax.axis_size(axis))]
    return lax.ppermute(value, axis, pairs)


def pack_kernel(edge, map_ref, tokens_ref, cots_ref, *rest):
    outs, sems = rest[:-1], rest[-1]
    me = lax.axis_index("fsdp")
    copies = []
    for mask, out in enumerate(outs):
        unit = me ^ mask
        for side, source in enumerate((tokens_ref, cots_ref)):
            start = pl.multiple_of(map_ref[side, unit] * edge, edge)
            copies.append(
                pltpu.make_async_copy(
                    source.at[0, :, pl.ds(start, edge)], out.at[side], sems.at[2 * mask + side]
                )
            )
    for copy in copies:
        copy.start()
    for copy in copies:
        copy.wait()


def packed(tokens, cotangent, block_map, edge):
    units = lax.axis_size("fsdp")
    rows = tokens.shape[1]
    return pl.pallas_call(
        functools.partial(pack_kernel, edge),
        out_shape=[jax.ShapeDtypeStruct((2, rows, edge), tokens.dtype)] * units,
        in_specs=[
            pl.BlockSpec(memory_space=pltpu.SMEM),
            pl.BlockSpec(memory_space=pltpu.HBM),
            pl.BlockSpec(memory_space=pltpu.HBM),
        ],
        out_specs=[pl.BlockSpec(memory_space=pltpu.VMEM)] * units,
        scratch_shapes=[pltpu.SemaphoreType.DMA((2 * units,))],
        compiler_params=pltpu.CompilerParams(vmem_limit_bytes=16 * 2**20),
    )(
        pltpu.with_memory_space_constraint(block_map.T, pltpu.HBM),
        pltpu.with_memory_space_constraint(tokens, pltpu.HBM),
        pltpu.with_memory_space_constraint(cotangent, pltpu.HBM),
    )


def run_terms(inputs_a, cots_b, tile_ref):
    factor = inputs_a.shape[-1] ** (-0.5)
    dot = functools.partial(lax.dot_general, preferred_element_type=jnp.float32)
    rows = (((1,), (0,)), ((), ()))
    rows_t = (((1,), (1,)), ((), ()))
    summed = (((0,), (0,)), ((), ()))
    gate_pre = factor * dot(inputs_a, tile_ref[0], rows)
    up_pre = factor * dot(inputs_a, tile_ref[1], rows)
    hidden_grad = factor * dot(cots_b, tile_ref[2], rows_t)
    sigmoid = jax.nn.sigmoid(gate_pre)
    activated = gate_pre * sigmoid
    hidden = (activated * up_pre).astype(jnp.bfloat16)
    gate_grad = (hidden_grad * up_pre * sigmoid * (1.0 + gate_pre * (1.0 - sigmoid))).astype(
        jnp.bfloat16
    )
    up_grad = (hidden_grad * activated).astype(jnp.bfloat16)
    return [
        (factor * dot(inputs_a, gate_grad, summed)).astype(jnp.bfloat16).astype(jnp.float32),
        (factor * dot(inputs_a, up_grad, summed)).astype(jnp.bfloat16).astype(jnp.float32),
        (factor * dot(hidden, cots_b, summed)).astype(jnp.bfloat16).astype(jnp.float32),
    ]


def step_kernel(runs, *refs):
    pieces = refs[:runs]
    tile_ref, partner_ref, first_ref, second_ref, new_tile, new_first, new_second = refs[runs:]
    grads = None
    for piece in pieces:
        terms = run_terms(piece[0], piece[1], tile_ref)
        grads = terms if grads is None else [a + b for a, b in zip(grads, terms)]
    for part, grad in enumerate(grads):
        weights = tile_ref[part].astype(jnp.float32)
        first = BETA_ONE * first_ref[part] + (1.0 - BETA_ONE) * grad
        second = BETA_TWO * second_ref[part] + (1.0 - BETA_TWO) * grad * grad
        mixed = 0.5 * (weights + partner_ref[part].astype(jnp.float32)) - STEP_RATE * (
            first / (jnp.sqrt(second) + EPSILON) + WEIGHT_DECAY * weights
        )
        new_tile[part] = mixed.astype(new_tile.dtype)
        new_first[part] = first
        new_second[part] = second


def body(tokens, cotangent, block_map, matching, tiles, first_moment, second_moment):
    units = lax.axis_size("fsdp")
    tile = tiles[0, 0]
    edge = tile.shape[-1]
    pieces = packed(tokens, cotangent, block_map, edge)
    arrived = [pieces[0]] + [exchanged(pieces[mask], "fsdp", mask) for mask in range(1, units)]
    offset = matching[0]
    partner = tile
    for bit_number in range(lax.axis_size("rep").bit_length() - 1):
        swapped = exchanged(partner, "rep", 2**bit_number)
        partner = jnp.where(offset >> bit_number & 1 == 1, swapped, partner)
    new_tile, new_first, new_second = pl.pallas_call(
        functools.partial(step_kernel, units),
        out_shape=[
            jax.ShapeDtypeStruct(tile.shape, tile.dtype),
            jax.ShapeDtypeStruct(tile.shape, jnp.float32),
            jax.ShapeDtypeStruct(tile.shape, jnp.float32),
        ],
        in_specs=[pl.BlockSpec(memory_space=pltpu.VMEM)] * (units + 4),
        out_specs=[pl.BlockSpec(memory_space=pltpu.VMEM)] * 3,
        compiler_params=pltpu.CompilerParams(vmem_limit_bytes=16 * 2**20),
    )(*arrived, tile, partner, first_moment[0, 0], second_moment[0, 0])
    return new_tile[None, None], new_first[None, None], new_second[None, None]


def solution(mesh):
    wide = P("rep", "fsdp", None)
    deep = P("rep", "fsdp", None, None, None)
    return jax.shard_map(
        body,
        mesh=mesh,
        in_specs=(wide, wide, P(), P(), deep, deep, deep),
        out_specs=(deep, deep, deep),
        check_vma=False,
    )
```

```python
import functools

import jax
import jax.numpy as jnp
from jax import lax
from jax.experimental import pallas as pl
from jax.experimental.pallas import tpu as pltpu
from jax.sharding import PartitionSpec as P


BETA_ONE = 0.9
BETA_TWO = 0.95
STEP_RATE = 0.02
WEIGHT_DECAY = 0.1
EPSILON = 1e-08
GROUP = 4

VMEM_SPEC = pl.BlockSpec(memory_space=pltpu.VMEM)
HBM_SPEC = pl.BlockSpec(memory_space=pltpu.HBM)
SMEM_SPEC = pl.BlockSpec(memory_space=pltpu.SMEM)
KERNEL_PARAMS = pltpu.CompilerParams(vmem_limit_bytes=16 * 2**20)


def exchanged(value, axis, mask):
    pairs = [(source, source ^ mask) for source in range(lax.axis_size(axis))]
    return lax.ppermute(value, axis, pairs)


def kernel_call(*args, **kwargs):
    def call(*operands):
        return pl.pallas_call(*args, compiler_params=KERNEL_PARAMS, **kwargs)(*operands)

    return call


def pack_kernel(edge, masks, map_ref, tokens_ref, cots_ref, *rest):
    outs, sems = rest[:-1], rest[-1]
    me = lax.axis_index("fsdp")
    copies = []
    for place, (mask, out) in enumerate(zip(masks, outs)):
        unit = me ^ mask
        for side, source in enumerate((tokens_ref, cots_ref)):
            start = pl.multiple_of(map_ref[side, unit] * edge, edge)
            copies.append(
                pltpu.make_async_copy(
                    source.at[0, :, pl.ds(start, edge)], out.at[side], sems.at[2 * place + side]
                )
            )
    for copy in copies:
        copy.start()
    for copy in copies:
        copy.wait()


def packed(masks, tokens, cotangent, map_t, edge):
    rows = tokens.shape[1]
    outs = kernel_call(
        functools.partial(pack_kernel, edge, masks),
        out_shape=[jax.ShapeDtypeStruct((2, rows, edge), tokens.dtype)] * len(masks),
        in_specs=[SMEM_SPEC, HBM_SPEC, HBM_SPEC],
        out_specs=[VMEM_SPEC] * len(masks),
        scratch_shapes=[pltpu.SemaphoreType.DMA((2 * len(masks),))],
    )(map_t, tokens, cotangent)
    return dict(zip(masks, outs))


def run_terms(inputs_a, cots_b, tile_ref):
    factor = inputs_a.shape[-1] ** (-0.5)
    dot = functools.partial(lax.dot_general, preferred_element_type=jnp.float32)
    rows = (((1,), (0,)), ((), ()))
    rows_t = (((1,), (1,)), ((), ()))
    summed = (((0,), (0,)), ((), ()))
    gate_pre = factor * dot(inputs_a, tile_ref[0], rows)
    up_pre = factor * dot(inputs_a, tile_ref[1], rows)
    hidden_grad = factor * dot(cots_b, tile_ref[2], rows_t)
    sigmoid = jax.nn.sigmoid(gate_pre)
    activated = gate_pre * sigmoid
    hidden = (activated * up_pre).astype(jnp.bfloat16)
    gate_grad = (hidden_grad * up_pre * sigmoid * (1.0 + gate_pre * (1.0 - sigmoid))).astype(
        jnp.bfloat16
    )
    up_grad = (hidden_grad * activated).astype(jnp.bfloat16)
    return [
        (factor * dot(inputs_a, gate_grad, summed)).astype(jnp.bfloat16).astype(jnp.float32),
        (factor * dot(inputs_a, up_grad, summed)).astype(jnp.bfloat16).astype(jnp.float32),
        (factor * dot(hidden, cots_b, summed)).astype(jnp.bfloat16).astype(jnp.float32),
    ]


def sum_kernel(runs, *refs):
    pieces, tile_ref, before, out = refs[:runs], refs[runs], refs[runs + 1 : -1], refs[-1]
    grads = [before[0][part] for part in range(out.shape[0])] if before else None
    for piece in pieces:
        terms = run_terms(piece[0], piece[1], tile_ref)
        grads = terms if grads is None else [a + b for a, b in zip(grads, terms)]
    for part, grad in enumerate(grads):
        out[part] = grad.astype(out.dtype)


def summed_terms(pieces, tile, before, dtype):
    operands = [*pieces, tile] + ([] if before is None else [before])
    return kernel_call(
        functools.partial(sum_kernel, len(pieces)),
        out_shape=jax.ShapeDtypeStruct(tile.shape, dtype),
        in_specs=[VMEM_SPEC] * len(operands),
        out_specs=VMEM_SPEC,
    )(*operands)


def step_kernel(others, *refs):
    sums = refs[: others + 1]
    tile_ref, partner_ref, first_ref, second_ref, new_tile, new_first, new_second = refs[
        others + 1 :
    ]
    for part in range(tile_ref.shape[0]):
        grad = sums[0][part]
        for other in sums[1:]:
            grad = grad + other[part].astype(jnp.float32)
        weights = tile_ref[part].astype(jnp.float32)
        first = BETA_ONE * first_ref[part] + (1.0 - BETA_ONE) * grad
        second = BETA_TWO * second_ref[part] + (1.0 - BETA_TWO) * grad * grad
        mixed = 0.5 * (weights + partner_ref[part].astype(jnp.float32)) - STEP_RATE * (
            first / (jnp.sqrt(second) + EPSILON) + WEIGHT_DECAY * weights
        )
        new_tile[part] = mixed.astype(new_tile.dtype)
        new_first[part] = first
        new_second[part] = second


def body(tokens, cotangent, block_map, matching, tiles, first_moment, second_moment):
    units = lax.axis_size("fsdp")
    group = min(GROUP, units)
    tile = tiles[0, 0]
    edge = tile.shape[-1]
    hbm = functools.partial(pltpu.with_memory_space_constraint, memory_space=pltpu.HBM)
    sources = (hbm(tokens), hbm(cotangent), hbm(block_map.T), edge)
    pieces = packed(range(units), *sources)

    def gathered(base):
        return [pieces[base]] + [
            exchanged(pieces[base + hop], "fsdp", hop)
            for hop in range(1, group)
        ]

    def reduced(base, weights, dtype):
        runs = gathered(base)
        half = max(1, group // 2)
        early = summed_terms(runs[:half], weights, None, jnp.float32)
        return summed_terms(runs[half:], weights, early, dtype)

    returned = []
    for base in range(group, units, group):
        weights = exchanged(tile, "fsdp", base)
        total = reduced(base, weights, tile.dtype)
        returned.append(exchanged(total, "fsdp", base))
    own = reduced(0, tile, jnp.float32)
    offset = matching[0]
    partner = tile
    for bit_number in range(lax.axis_size("rep").bit_length() - 1):
        swapped = exchanged(partner, "rep", 2**bit_number)
        partner = jnp.where(offset >> bit_number & 1 == 1, swapped, partner)
    operands = [own, *returned, tile, partner, first_moment[0, 0], second_moment[0, 0]]
    new_tile, new_first, new_second = kernel_call(
        functools.partial(step_kernel, len(returned)),
        out_shape=[
            jax.ShapeDtypeStruct(tile.shape, tile.dtype),
            jax.ShapeDtypeStruct(tile.shape, jnp.float32),
            jax.ShapeDtypeStruct(tile.shape, jnp.float32),
        ],
        in_specs=[VMEM_SPEC] * len(operands),
        out_specs=[VMEM_SPEC] * 3,
    )(*operands)
    return new_tile[None, None], new_first[None, None], new_second[None, None]


def solution(mesh):
    wide = P("rep", "fsdp", None)
    deep = P("rep", "fsdp", None, None, None)
    return jax.shard_map(
        body,
        mesh=mesh,
        in_specs=(wide, wide, P(), P(), deep, deep, deep),
        out_specs=(deep, deep, deep),
        check_vma=False,
    )
```

```python
import functools

import jax
import jax.numpy as jnp
from jax import lax
from jax.experimental import pallas as pl
from jax.experimental.pallas import tpu as pltpu
from jax.sharding import PartitionSpec as P


BETA_ONE = 0.9
BETA_TWO = 0.95
STEP_RATE = 0.02
WEIGHT_DECAY = 0.1
EPSILON = 1e-08
CORES = 2
GROUP = 4

VMEM_SPEC = pl.BlockSpec(memory_space=pltpu.VMEM)
HBM_SPEC = pl.BlockSpec(memory_space=pltpu.HBM)
SMEM_SPEC = pl.BlockSpec(memory_space=pltpu.SMEM)
KERNEL_PARAMS = pltpu.CompilerParams(vmem_limit_bytes=16 * 2**20)


def exchanged(value, axis, mask):
    pairs = [(source, source ^ mask) for source in range(lax.axis_size(axis))]
    return lax.ppermute(value, axis, pairs)


def kernel_call(*args, **kwargs):
    def call(*operands):
        return pl.pallas_call(*args, compiler_params=KERNEL_PARAMS, **kwargs)(*operands)

    return call


def pack_kernel(edge, groups, map_ref, tokens_ref, cots_ref, *rest):
    outs, sems = rest[:-1], rest[-1]
    me = lax.axis_index("fsdp")
    copies = []
    for masks, out in zip(groups, outs):
        for place, mask in enumerate(masks):
            unit = me ^ mask
            for side, source in enumerate((tokens_ref, cots_ref)):
                start = pl.multiple_of(map_ref[side, unit] * edge, edge)
                copies.append(
                    pltpu.make_async_copy(
                        source.at[0, :, pl.ds(start, edge)],
                        out.at[place, side],
                        sems.at[len(copies)],
                    )
                )
    for copy in copies:
        copy.start()
    for copy in copies:
        copy.wait()


def packed(groups, tokens, cotangent, map_t, edge):
    rows = tokens.shape[1]
    return kernel_call(
        functools.partial(pack_kernel, edge, groups),
        out_shape=[
            jax.ShapeDtypeStruct((len(masks), 2, rows, edge), tokens.dtype) for masks in groups
        ],
        in_specs=[SMEM_SPEC, HBM_SPEC, HBM_SPEC],
        out_specs=[VMEM_SPEC] * len(groups),
        scratch_shapes=[pltpu.SemaphoreType.DMA((2 * sum(map(len, groups)),))],
    )(map_t, tokens, cotangent)


def run_terms(inputs_a, cots_b, wide_tile, down_tile):
    edge = inputs_a.shape[-1]
    factor = edge ** (-0.5)
    dot = functools.partial(lax.dot_general, preferred_element_type=jnp.float32)
    rows = (((1,), (0,)), ((), ()))
    rows_t = (((1,), (1,)), ((), ()))
    summed = (((0,), (0,)), ((), ()))
    pre = factor * dot(inputs_a, wide_tile, rows)
    gate_pre, up_pre = pre[:, :edge], pre[:, edge:]
    hidden_grad = factor * dot(cots_b, down_tile, rows_t)
    sigmoid = jax.nn.sigmoid(gate_pre)
    activated = gate_pre * sigmoid
    hidden = (activated * up_pre).astype(jnp.bfloat16)
    gate_grad = (hidden_grad * up_pre * sigmoid * (1.0 + gate_pre * (1.0 - sigmoid))).astype(
        jnp.bfloat16
    )
    up_grad = (hidden_grad * activated).astype(jnp.bfloat16)
    wide_grad = dot(inputs_a, jnp.concatenate([gate_grad, up_grad], axis=1), summed)
    down_grad = dot(hidden, cots_b, summed)
    terms = (wide_grad[:, :edge], wide_grad[:, edge:], down_grad)
    return [(factor * term).astype(jnp.bfloat16).astype(jnp.float32) for term in terms]


def sum_kernel(places, *refs):
    runs = len(places)
    pieces, tile_ref, before, out = refs[:runs], refs[runs], refs[runs + 1 : -1], refs[-1]
    grads = [before[0][part] for part in range(out.shape[0])] if before else None
    wide_tile = jnp.concatenate([tile_ref[0], tile_ref[1]], axis=1)
    for place, piece in zip(places, pieces):
        terms = run_terms(piece[place, 0], piece[place, 1], wide_tile, tile_ref[2])
        grads = terms if grads is None else [a + b for a, b in zip(grads, terms)]
    for part, grad in enumerate(grads):
        out[part] = grad.astype(out.dtype)


def summed_terms(runs, tile, before, dtype):
    pieces, places = zip(*runs)
    operands = [*pieces, tile] + ([] if before is None else [before])
    return kernel_call(
        functools.partial(sum_kernel, places),
        out_shape=jax.ShapeDtypeStruct(tile.shape, dtype),
        in_specs=[VMEM_SPEC] * len(operands),
        out_specs=VMEM_SPEC,
    )(*operands)


def step_kernel(others, *refs):
    sums = refs[: others + 1]
    tile_ref, partner_ref, first_ref, second_ref, new_tile, new_first, new_second = refs[
        others + 1 :
    ]
    for part in range(tile_ref.shape[0]):
        grad = sums[0][part]
        for other in sums[1:]:
            grad = grad + other[part].astype(jnp.float32)
        weights = tile_ref[part].astype(jnp.float32)
        first = BETA_ONE * first_ref[part] + (1.0 - BETA_ONE) * grad
        second = BETA_TWO * second_ref[part] + (1.0 - BETA_TWO) * grad * grad
        mixed = 0.5 * (weights + partner_ref[part].astype(jnp.float32)) - STEP_RATE * (
            first / (jnp.sqrt(second) + EPSILON) + WEIGHT_DECAY * weights
        )
        new_tile[part] = mixed.astype(new_tile.dtype)
        new_first[part] = first
        new_second[part] = second


def body(tokens, cotangent, block_map, matching, tiles, first_moment, second_moment):
    units = lax.axis_size("fsdp")
    group = min(GROUP, units)
    tile = tiles[0, 0]
    edge = tile.shape[-1]
    hbm = functools.partial(pltpu.with_memory_space_constraint, memory_space=pltpu.HBM)
    sources = (hbm(tokens), hbm(cotangent), hbm(block_map.T), edge)
    cores = min(CORES, units)
    bases = range(0, units, group)
    hops = range(cores, group)
    local = [[base + hop for base in bases] for hop in range(cores)]
    afar = [[base + hop] for base in bases[1:] for hop in hops]
    own = [[hop] for hop in hops]
    first, rest = afar, [*own, *local]
    groups = [*first, *rest]
    blocks = packed(first, *sources) if first else []
    blocks = [*blocks, *packed(rest, *sources)]
    held = {}
    for masks, piece in zip(groups, blocks):
        hop = masks[0] % group
        if hop:
            piece = exchanged(piece, "fsdp", hop)
        for place, mask in enumerate(masks):
            held[mask] = (piece, place)

    def gathered(base):
        return [held[base + hop] for hop in range(group)]

    def reduced(base, weights, dtype):
        runs = gathered(base)
        half = group - 1
        early = summed_terms(runs[:half], weights, None, jnp.float32)
        return summed_terms(runs[half:], weights, early, dtype)

    returned = []
    for base in range(group, units, group):
        weights = exchanged(tile, "fsdp", base)
        total = reduced(base, weights, tile.dtype)
        returned.append(exchanged(total, "fsdp", base))
    own = reduced(0, tile, jnp.float32)
    offset = matching[0]
    partner = tile
    for bit_number in range(lax.axis_size("rep").bit_length() - 1):
        swapped = exchanged(partner, "rep", 2**bit_number)
        partner = jnp.where(offset >> bit_number & 1 == 1, swapped, partner)
    operands = [own, *returned, tile, partner, first_moment[0, 0], second_moment[0, 0]]
    new_tile, new_first, new_second = kernel_call(
        functools.partial(step_kernel, len(returned)),
        out_shape=[
            jax.ShapeDtypeStruct(tile.shape, tile.dtype),
            jax.ShapeDtypeStruct(tile.shape, jnp.float32),
            jax.ShapeDtypeStruct(tile.shape, jnp.float32),
        ],
        in_specs=[VMEM_SPEC] * len(operands),
        out_specs=[VMEM_SPEC] * 3,
    )(*operands)
    return new_tile[None, None], new_first[None, None], new_second[None, None]


def solution(mesh):
    wide = P("rep", "fsdp", None)
    deep = P("rep", "fsdp", None, None, None)
    return jax.shard_map(
        body,
        mesh=mesh,
        in_specs=(wide, wide, P(), P(), deep, deep, deep),
        out_specs=(deep, deep, deep),
        check_vma=False,
    )
```

```python
import functools

import jax
import jax.numpy as jnp
from jax import lax
from jax.experimental import pallas as pl
from jax.experimental.pallas import tpu as pltpu
from jax.sharding import PartitionSpec as P


BETA_ONE = 0.9
BETA_TWO = 0.95
STEP_RATE = 0.02
WEIGHT_DECAY = 0.1
EPSILON = 1e-08
CORES = 2
GROUP = 4

VMEM_SPEC = pl.BlockSpec(memory_space=pltpu.VMEM)
HBM_SPEC = pl.BlockSpec(memory_space=pltpu.HBM)
SMEM_SPEC = pl.BlockSpec(memory_space=pltpu.SMEM)
KERNEL_PARAMS = pltpu.CompilerParams(vmem_limit_bytes=16 * 2**20)


def exchanged(value, axis, mask):
    pairs = [(source, source ^ mask) for source in range(lax.axis_size(axis))]
    return lax.ppermute(value, axis, pairs)


def kernel_call(*args, **kwargs):
    def call(*operands):
        return pl.pallas_call(*args, compiler_params=KERNEL_PARAMS, **kwargs)(*operands)

    return call


def pack_kernel(edge, groups, map_ref, tokens_ref, cots_ref, *rest):
    outs, sems = rest[:-1], rest[-1]
    me = lax.axis_index("fsdp")
    copies = []
    for masks, out in zip(groups, outs):
        for place, mask in enumerate(masks):
            unit = me ^ mask
            for side, source in enumerate((tokens_ref, cots_ref)):
                start = pl.multiple_of(map_ref[side, unit] * edge, edge)
                copies.append(
                    pltpu.make_async_copy(
                        source.at[0, :, pl.ds(start, edge)],
                        out.at[place, side],
                        sems.at[len(copies)],
                    )
                )
    for copy in copies:
        copy.start()
    for copy in copies:
        copy.wait()


def packed(groups, tokens, cotangent, map_t, edge):
    rows = tokens.shape[1]
    return kernel_call(
        functools.partial(pack_kernel, edge, groups),
        out_shape=[
            jax.ShapeDtypeStruct((len(masks), 2, rows, edge), tokens.dtype) for masks in groups
        ],
        in_specs=[SMEM_SPEC, HBM_SPEC, HBM_SPEC],
        out_specs=[VMEM_SPEC] * len(groups),
        scratch_shapes=[pltpu.SemaphoreType.DMA((2 * sum(map(len, groups)),))],
    )(map_t, tokens, cotangent)


def run_terms(inputs_a, cots_b, wide_tile, down_tile):
    edge = inputs_a.shape[-1]
    factor = edge ** (-0.5)
    dot = functools.partial(lax.dot_general, preferred_element_type=jnp.float32)
    rows = (((1,), (0,)), ((), ()))
    rows_t = (((1,), (1,)), ((), ()))
    summed = (((0,), (0,)), ((), ()))
    pre = factor * dot(inputs_a, wide_tile, rows)
    gate_pre, up_pre = pre[:, :edge], pre[:, edge:]
    hidden_grad = factor * dot(cots_b, down_tile, rows_t)
    sigmoid = jax.nn.sigmoid(gate_pre)
    activated = gate_pre * sigmoid
    hidden = (activated * up_pre).astype(jnp.bfloat16)
    gate_grad = (hidden_grad * up_pre * sigmoid * (1.0 + gate_pre * (1.0 - sigmoid))).astype(
        jnp.bfloat16
    )
    up_grad = (hidden_grad * activated).astype(jnp.bfloat16)
    wide_grad = dot(inputs_a, jnp.concatenate([gate_grad, up_grad], axis=1), summed)
    down_grad = dot(hidden, cots_b, summed)
    terms = (wide_grad[:, :edge], wide_grad[:, edge:], down_grad)
    return list(terms)


def sum_kernel(places, *refs):
    runs = len(places)
    pieces, tile_ref, before, out = refs[:runs], refs[runs], refs[runs + 1 : -1], refs[-1]
    factor = tile_ref.shape[-1] ** (-0.5)
    grads = None
    wide_tile = jnp.concatenate([tile_ref[0], tile_ref[1]], axis=1)
    for place, piece in zip(places, pieces):
        terms = run_terms(piece[place, 0], piece[place, 1], wide_tile, tile_ref[2])
        grads = terms if grads is None else [a + b for a, b in zip(grads, terms)]
    for part, grad in enumerate(grads):
        total = factor * grad
        if before:
            total = total + before[0][part]
        out[part] = total.astype(out.dtype)


def summed_terms(runs, tile, before, dtype):
    pieces, places = zip(*runs)
    operands = [*pieces, tile] + ([] if before is None else [before])
    return kernel_call(
        functools.partial(sum_kernel, places),
        out_shape=jax.ShapeDtypeStruct(tile.shape, dtype),
        in_specs=[VMEM_SPEC] * len(operands),
        out_specs=VMEM_SPEC,
    )(*operands)


def step_kernel(others, *refs):
    sums = refs[: others + 1]
    tile_ref, partner_ref, first_ref, second_ref = refs[others + 1 : others + 5]
    targets = refs[others + 5 : others + 8]
    held, sems = refs[others + 8 : others + 11], refs[others + 11]
    copies = []
    for part in range(tile_ref.shape[0]):
        grad = sums[0][part]
        for other in sums[1:]:
            grad = grad + other[part].astype(jnp.float32)
        weights = tile_ref[part].astype(jnp.float32)
        first = BETA_ONE * first_ref[part] + (1.0 - BETA_ONE) * grad
        second = BETA_TWO * second_ref[part] + (1.0 - BETA_TWO) * grad * grad
        mixed = 0.5 * (weights + partner_ref[part].astype(jnp.float32)) - STEP_RATE * (
            first / (jnp.sqrt(second) + EPSILON) + WEIGHT_DECAY * weights
        )
        for place, value in enumerate((mixed.astype(tile_ref.dtype), first, second)):
            held[place][part] = value
            copy = pltpu.make_async_copy(
                held[place].at[part], targets[place].at[part], sems.at[place, part]
            )
            copy.start()
            copies.append(copy)
    for copy in copies:
        copy.wait()


def body(tokens, cotangent, block_map, matching, tiles, first_moment, second_moment):
    units = lax.axis_size("fsdp")
    group = min(GROUP, units)
    tile = tiles[0, 0]
    edge = tile.shape[-1]
    hbm = functools.partial(pltpu.with_memory_space_constraint, memory_space=pltpu.HBM)
    sources = (hbm(tokens), hbm(cotangent), hbm(block_map.T), edge)
    cores = min(CORES, units)
    bases = range(0, units, group)
    hops = range(cores, group)
    local = [[base + hop for base in bases] for hop in range(cores)]
    afar = [[base + hop] for base in bases[1:] for hop in hops]
    own = [[hop] for hop in hops]
    first, rest = afar, [*own, *local]
    groups = [*first, *rest]
    blocks = packed(first, *sources) if first else []
    blocks = [*blocks, *packed(rest, *sources)]
    held = {}
    for masks, piece in zip(groups, blocks):
        hop = masks[0] % group
        if hop:
            piece = exchanged(piece, "fsdp", hop)
        for place, mask in enumerate(masks):
            held[mask] = (piece, place)

    def gathered(base):
        return [held[base + hop] for hop in range(group)]

    def reduced(base, weights, dtype):
        runs = gathered(base)
        half = group - 1
        early = summed_terms(runs[:half], weights, None, jnp.float32)
        return summed_terms(runs[half:], weights, early, dtype)

    returned = []
    for base in range(group, units, group):
        weights = exchanged(tile, "fsdp", base)
        total = reduced(base, weights, tile.dtype)
        returned.append(exchanged(total, "fsdp", base))
    own = reduced(0, tile, jnp.float32)
    offset = matching[0]
    partner = tile
    for bit_number in range(lax.axis_size("rep").bit_length() - 1):
        swapped = exchanged(partner, "rep", 2**bit_number)
        partner = jnp.where(offset >> bit_number & 1 == 1, swapped, partner)
    operands = [own, *returned, tile, partner, first_moment[0, 0], second_moment[0, 0]]
    new_tile, new_first, new_second = kernel_call(
        functools.partial(step_kernel, len(returned)),
        out_shape=[
            jax.ShapeDtypeStruct(tile.shape, tile.dtype),
            jax.ShapeDtypeStruct(tile.shape, jnp.float32),
            jax.ShapeDtypeStruct(tile.shape, jnp.float32),
        ],
        in_specs=[VMEM_SPEC] * len(operands),
        out_specs=[HBM_SPEC] * 3,
        scratch_shapes=[
            pltpu.VMEM(tile.shape, tile.dtype),
            pltpu.VMEM(tile.shape, jnp.float32),
            pltpu.VMEM(tile.shape, jnp.float32),
            pltpu.SemaphoreType.DMA((3, tile.shape[0])),
        ],
    )(*operands)
    return new_tile[None, None], new_first[None, None], new_second[None, None]


def solution(mesh):
    wide = P("rep", "fsdp", None)
    deep = P("rep", "fsdp", None, None, None)
    return jax.shard_map(
        body,
        mesh=mesh,
        in_specs=(wide, wide, P(), P(), deep, deep, deep),
        out_specs=(deep, deep, deep),
        check_vma=False,
    )
```
